32 devices in a mesh: stream: 8 (over y, x, core), tp: 4 (over z).
Axes of the slice: x: 2, y: 2, z: 4, core: 2. Of those that a mesh axis runs over, the one named last changes fastest.
Arguments:
- tokens: bfloat16 [12288, 3072], P('stream', 'tp'), may hold values from -6 to 6
- qkv_weight: bfloat16 [3072, 3, 2048], P('stream', None, 'tp'), may hold values from -0.109375 to 0.109375
- gate_weight: bfloat16 [3072, 2048], P('stream', 'tp'), may hold values from -0.109375 to 0.109375
- out_weight: bfloat16 [2048, 3072], P('tp', 'stream'), may hold values from -0.125 to 0.125
- log_decay: float32 [32, 12288], P('tp', 'stream'), may hold values from -1 to 0
- states: float32 [96, 32, 64, 64], P('stream', 'tp'), may hold values from -48 to 48
- dest_slot: int32 [96], P('stream'), may hold values from 0 to 95, as said below
- valid: int32 [96], P('stream'), may hold values from 1 to 128
Outputs:
- mixed: bfloat16 [12288, 3072], P('stream', 'tp')
- new_states: float32 [96, 32, 64, 64], P('stream', 'tp')
The draws below stay inside these ranges and needn't reach their ends.
Inputs may be any that keep to these rules, and one draw needn't show every extreme that they name: dest_slot is a permutation of the streams; of the 12 streams of one device, at most 2 have new positions on any one device, and that many do for some pair of devices.
All inputs are finite; a program needn't handle non-finite values.
Results may differ from the reference program's by a relative error of at most 0.0058.
Values may be sent and summed in bfloat16 or wider, within the bound.
A program may use at most 128 MiB of HBM per device.

```python
import math
import jax
import jax.numpy as jnp
from jax import lax

D = 3072
NUM_ATTENDERS = 32
HD = 64
WINDOW_LENGTH = 128
SD = 12
NUM_SEQUENCES = 96
TOKENS = 12288


def draw_log_decay(key, part):
    lookup_vectors = jax.random.split(key, 5)
    forgetting_speed = jnp.exp(jax.random.uniform(lookup_vectors[0], (NUM_ATTENDERS, 1, 1), jnp.float32, math.log(0.2 / WINDOW_LENGTH), math.log(1.0 / 30.0)))
    multiplier_value = jnp.exp(jax.random.uniform(lookup_vectors[1], (1, NUM_SEQUENCES, 1), jnp.float32, math.log(0.5), math.log(2.0)))
    noise_offset = jax.random.uniform(lookup_vectors[2], (NUM_ATTENDERS, NUM_SEQUENCES, WINDOW_LENGTH), jnp.float32, 0.6, 1.4)
    sequence_bundles = jax.random.bernoulli(lookup_vectors[3], 2.0 / WINDOW_LENGTH, (NUM_ATTENDERS, NUM_SEQUENCES, WINDOW_LENGTH)).astype(jnp.float32)
    network_level = jax.random.uniform(lookup_vectors[4], (NUM_ATTENDERS, NUM_SEQUENCES, WINDOW_LENGTH), jnp.float32, 0.22, 0.69)
    overall_number = forgetting_speed * multiplier_value * noise_offset + sequence_bundles * network_level
    return (-overall_number).reshape(NUM_ATTENDERS, NUM_SEQUENCES * WINDOW_LENGTH).astype(jnp.float32)


def draw_dest_slot(key, part):
    node_count = NUM_SEQUENCES // SD
    lookup_vectors = jax.random.split(key, 3)
    first_perm = jax.random.permutation(lookup_vectors[0], node_count)
    second_perm = jax.random.permutation(lookup_vectors[1], node_count)
    slot_keys = jax.random.split(lookup_vectors[2], node_count)
    slot_perm = jax.vmap(lambda k: jax.random.permutation(k, SD))(slot_keys)
    index = jnp.arange(NUM_SEQUENCES, dtype=jnp.int32)
    device = index // SD
    within = index % SD
    target = second_perm[(first_perm[device] + within) % node_count]
    return (target * SD + slot_perm[target, within]).astype(jnp.int32)


def draw_valid(key, part):
    lookup_vectors = jax.random.split(key, 3)
    counts = jax.random.randint(lookup_vectors[0], (NUM_SEQUENCES,), 1, WINDOW_LENGTH + 1, dtype=jnp.int32)
    first_pos = jax.random.randint(lookup_vectors[1], (), 0, NUM_SEQUENCES, dtype=jnp.int32)
    second_pos = (first_pos + 1 + jax.random.randint(lookup_vectors[2], (), 0, NUM_SEQUENCES - 1, dtype=jnp.int32)) % NUM_SEQUENCES
    return counts.at[first_pos].set(WINDOW_LENGTH).at[second_pos].set(1).astype(jnp.int32)


def steps_of(rng, shape, shards, low, top_value):
    def one(position, parts):
        draws = jax.random.uniform(jax.random.fold_in(jax.random.fold_in(rng, 6), position), (parts,), jnp.float32, low / len(shards), top_value / len(shards))
        return jnp.repeat(jnp.exp(draws), shape[position] // parts).reshape((-1,) + (1,) * (len(shape) - position - 1))

    factor_of = one(*shards[0])
    for cut in shards[1:]:
        factor_of = factor_of * one(*cut)
    return factor_of


def noise(own_key, shape, width, limit, shards=(), kind=jnp.bfloat16):
    values = jax.random.normal(own_key, shape, jnp.float32) * width
    if len(shards) > 0:
        values = steps_of(own_key, shape, shards, -0.22, 0.18) * values
    return jnp.clip(values, min=-limit, max=limit).astype(kind)


def setup_inputs(seed: int = 0) -> dict:
    splits = jax.random.split(jax.random.key(seed), 9)
    tokens = noise(splits[0], (TOKENS, D), 1.0, 6.0, ((0, 8), (1, 4)))
    qkv_weight = noise(splits[1], (D, 3, NUM_ATTENDERS * HD), D ** -0.5, 0.109375, ((0, 8), (2, 4)))
    gate_weight = noise(splits[2], (D, NUM_ATTENDERS * HD), D ** -0.5, 0.109375, ((0, 8), (1, 4)))
    out_weight = noise(splits[3], (NUM_ATTENDERS * HD, D), (NUM_ATTENDERS * HD) ** -0.5, 0.125, ((0, 4), (1, 8)))
    log_decay = draw_log_decay(jax.random.fold_in(splits[8], 71), 0)
    states = noise(splits[5], (NUM_SEQUENCES, NUM_ATTENDERS, HD, HD), 8.0, 48.0, ((0, 8), (1, 4)), jnp.float32)
    dest_slot = draw_dest_slot(jax.random.fold_in(splits[8], 71), 0)
    valid = draw_valid(jax.random.fold_in(splits[8], 71), 0)
    return {"tokens": tokens, "qkv_weight": qkv_weight, "gate_weight": gate_weight, "out_weight": out_weight, "log_decay": log_decay, "states": states, "dest_slot": dest_slot, "valid": valid}


def core(projected, gate_sum, decay_log, old_state, valid_rows):
    streams = old_state.shape[0]
    heads = old_state.shape[1]
    rows = projected.shape[0]
    length = rows // streams
    activated = jax.nn.silu(projected).astype(jnp.bfloat16).reshape(streams, length, 3, heads, HD)
    positions = jnp.arange(length, dtype=jnp.int32)
    live = positions[None, :] < valid_rows[:, None]
    live_half = live.astype(jnp.bfloat16)[:, :, None, None]
    live_full = live.astype(jnp.float32)
    query = activated[:, :, 0]
    lookup_vectors = activated[:, :, 1] * live_half
    values = activated[:, :, 2] * live_half
    decay = decay_log.reshape(heads, streams, length).transpose(1, 0, 2) * live_full[:, None, :]
    cumulative = jnp.cumsum(decay, axis=2)
    query_full = query.astype(jnp.float32)
    keys_full = lookup_vectors.astype(jnp.float32)
    values_full = values.astype(jnp.float32)
    scores = jnp.einsum('sthd,suhd->shtu', query_full, keys_full)
    causal = positions[:, None] >= positions[None, :]
    gap = cumulative[:, :, :, None] - cumulative[:, :, None, :]
    weights = jnp.where(causal, jnp.exp(jnp.minimum(gap, 0.0)), 0.0)
    probs = (scores * weights).astype(jnp.bfloat16)
    intra = jnp.einsum('shtu,suhd->sthd', probs.astype(jnp.float32), values_full)
    carried = jnp.einsum('sthd,shde->sthe', query_full, old_state, precision=lax.Precision.HIGHEST)
    carried = carried * jnp.exp(cumulative).transpose(0, 2, 1)[:, :, :, None]
    attended = intra + carried
    final_log = cumulative[:, :, length - 1:]
    weighted_keys = keys_full * jnp.exp(final_log - cumulative).transpose(0, 2, 1)[:, :, :, None]
    updated = jnp.exp(final_log)[:, :, :, None] * old_state + jnp.einsum('sthd,sthe->shde', weighted_keys, values_full, precision=lax.Precision.HIGHEST)
    mean_square = lax.optimization_barrier(jnp.mean(attended * attended, axis=-1, keepdims=True))
    normed = attended * lax.rsqrt(mean_square + 1e-05)
    gates = jax.nn.sigmoid(gate_sum).reshape(streams, length, heads, HD)
    hidden = (normed * gates * live_full[:, :, None, None]).astype(jnp.bfloat16).reshape(rows, heads * HD)
    return (hidden, updated)

def reference(tokens, qkv_weight, gate_weight, out_weight, log_decay, states, dest_slot, valid):
    moved = jnp.zeros_like(states).at[dest_slot].set(states)
    blocks = NUM_SEQUENCES // SD
    flat_qkv = qkv_weight.reshape(D, 3 * NUM_ATTENDERS * HD)

    def run(item):
        rows_x, decay_rows, old_state, valid_rows = item
        projected = jnp.dot(rows_x, flat_qkv, preferred_element_type=jnp.float32)
        gate_sum = jnp.dot(rows_x, gate_weight, preferred_element_type=jnp.float32)
        hidden, updated = core(projected, gate_sum, decay_rows, old_state, valid_rows)
        mixed = jnp.dot(hidden, out_weight, preferred_element_type=jnp.float32).astype(jnp.bfloat16)
        return (mixed, updated)
    mixed, updated = lax.map(run, (tokens.reshape(blocks, SD * WINDOW_LENGTH, D), log_decay.reshape(NUM_ATTENDERS, blocks, SD * WINDOW_LENGTH).transpose(1, 0, 2), moved.reshape(blocks, SD, NUM_ATTENDERS, HD, HD), valid.reshape(blocks, SD)))
    return (mixed.reshape(TOKENS, D), updated.reshape(NUM_SEQUENCES, NUM_ATTENDERS, HD, HD))
```

```python
import functools
import math

import jax
import jax.numpy as jnp
from jax import lax
from jax.experimental import pallas as pl
from jax.experimental.pallas import tpu as pltpu
from jax.sharding import PartitionSpec as P

HD = 64
WINDOW_LENGTH = 128
PLANES = 4
CHUNK_STREAMS = 2
MESH = pl.DeviceIdType.MESH


def remote(src, dst, send, recv, target):
    return pltpu.make_async_remote_copy(
        src_ref=src, dst_ref=dst, send_sem=send, recv_sem=recv, device_id=target, device_id_type=MESH
    )


def product(a, b, left=1, right=0):
    return lax.dot_general(a, b, (((left,), (right,)), ((), ())), preferred_element_type=jnp.float32)


def halves(x):
    high = x.astype(jnp.bfloat16)
    return high, (x - high.astype(jnp.float32)).astype(jnp.bfloat16)


def layer_kernel(
    count,
    index_ref,
    valid_ref,
    t_hbm,
    w_hbm,
    o_hbm,
    s_hbm,
    label_hbm,
    decay_ref,
    mixed_hbm,
    updated_hbm,
    tok,
    weight,
    hidden,
    obuf,
    held,
    outgoing,
    incoming,
    labels,
    places,
    projected,
    staged,
    updated,
    local,
    recv_t,
    send_up,
    send_down,
    recv_w,
    send_w1,
    send_w2,
    send_ws,
    recv_s,
    send_s,
    recv_l,
    send_l,
    recv_o,
    send_o,
    recv_b,
    send_ba,
    send_bb,
    send_bs,
    recv_h,
    send_h,
    send_f,
    recv_m,
    send_m,
    local_m,
):
    me = lax.axis_index("stream")
    z = lax.axis_index("tp")
    core, chip = me % 2, me // 2
    chips = count // 2
    side = math.isqrt(chips)
    x, y = chip % side, chip // side
    streams, heads = held.shape[:2]
    width = heads * HD
    pairs = heads // 2
    features = t_hbm.shape[1]
    depth = w_hbm.shape[0]
    capacity = outgoing.shape[0] // count
    rows = CHUNK_STREAMS * WINDOW_LENGTH
    n = streams // CHUNK_STREAMS
    per = count // PLANES
    half = z // 2
    first_half = count // 2
    is_mid = (z == 1) | (z == 2)
    is_end = (z == 0) | (z == 3)
    outer = 3 * half
    other_mid = 2 - half
    sibling = (me + 1 - 2 * core, z)

    def device(cx, cy):
        return (cy * side + cx) * 2 + core

    own_tok = tok.at[:, pl.ds(pl.multiple_of(z * features, features), features)]
    load_t = pltpu.make_async_copy(t_hbm, own_tok, local.at[0])
    load_t.start()
    own_w = weight.at[pl.ds(pl.multiple_of(me * depth, depth), depth)]
    load_w = pltpu.make_async_copy(w_hbm, own_w, local.at[1])
    load_w.start()
    load_s = pltpu.make_async_copy(s_hbm, held, local.at[2])
    load_s.start()
    barrier = pltpu.get_barrier_semaphore()

    @pl.loop(1, count)
    def _(d):
        pl.semaphore_signal(barrier, inc=1, device_id=((me + d) % count, z), device_id_type=MESH)

    for d in range(1, PLANES):
        pl.semaphore_signal(barrier, inc=1, device_id=(me, (z + d) % PLANES), device_id_type=MESH)
    pl.semaphore_wait(barrier, count - 1 + PLANES - 1)

    def token_slot(c, f):
        return tok.at[
            pl.ds(pl.multiple_of(c * rows, rows), rows),
            pl.ds(pl.multiple_of(f * features, features), features),
        ]

    def token_up(c, f):
        slot = token_slot(c, f)
        return remote(slot, slot, send_up.at[c, f], recv_t.at[c, f], (me, z + 1))

    def token_down(c, f):
        slot = token_slot(c, f)
        return remote(slot, slot, send_down.at[c, f], recv_t.at[c, f], (me, z - 1))

    def send_own(c):
        @pl.when(z < PLANES - 1)
        def _():
            token_up(c, z).start()

        @pl.when(z > 0)
        def _():
            token_down(c, z).start()

    def arrive(c, hops):
        @pl.when(z >= hops)
        def _():
            f = z - hops
            token_down(c, f).wait_recv()

            @pl.when(z < PLANES - 1)
            def _():
                token_up(c, f).start()

        @pl.when(z + hops < PLANES)
        def _():
            f = z + hops
            token_up(c, f).wait_recv()

            @pl.when(z > 0)
            def _():
                token_down(c, f).start()

    def first_peer(d):
        return ((x + d * (1 - core)) % side, (y + d * core) % side)

    def second_peer(d):
        return ((x + d * core) % side, (y + d * (1 - core)) % side)

    def weight_slot(source):
        return weight.at[pl.ds(pl.multiple_of(source * depth, depth), depth)]

    def weight_copy(source, send, target):
        slot = weight_slot(source)
        return remote(slot, slot, send, recv_w.at[source], target)

    def first_source(d):
        px, py = first_peer(-d)
        return device(px, py)

    def second_source(d, e):
        sx, sy = (x - d * core) % side, (y - d * (1 - core)) % side
        return device((sx - e * (1 - core)) % side, (sy - e * core) % side)

    def first_copy(d):
        px, py = first_peer(d)
        return weight_copy(me, send_w1.at[d], (device(px, py), z))

    def second_copy(source, d, e):
        px, py = second_peer(d)
        return weight_copy(source, send_w2.at[d, e], (device(px, py), z))

    def sibling_copy(source):
        return weight_copy(source, send_ws.at[source], sibling)

    def weights_start():
        for d in range(1, side):
            first_copy(d).start()
        for d in range(1, side):
            second_copy(me, d, 0).start()
        sibling_copy(me).start()

    def weights_first():
        for e in range(1, side):
            source = first_source(e)
            sibling_copy(source).wait_recv()
            for d in range(1, side):
                second_copy(source, d, e).start()
            sibling_copy(source).start()

    def weights_second():
        for d in range(1, side):
            for e in range(side):
                source = second_source(d, e)
                sibling_copy(source).wait_recv()
                sibling_copy(source).start()

    def weights_last():
        for c in range(chips):
            sibling_copy(2 * c + 1 - core).wait_recv()

    def slots_of(buffer, d):
        return buffer.at[pl.ds(d * capacity, capacity)]

    def states_copy(d):
        target = (me + d) % count
        return remote(
            slots_of(outgoing, target), slots_of(incoming, me), send_s.at[d], recv_s.at[d], (target, z)
        )

    def label_copy(d):
        target = (me + d) % count
        return remote(label_hbm.at[target], labels.at[me], send_l.at[d], recv_l.at[d], (target, z))

    keep_states = pltpu.make_async_copy(slots_of(outgoing, me), slots_of(incoming, me), local.at[3])
    keep_label = pltpu.make_async_copy(label_hbm.at[me], labels.at[me], local.at[4])
    read_labels = pltpu.make_async_copy(labels, places, local.at[5])

    def states_start():
        @pl.loop(1, count)
        def _(d):
            label_copy(d).start()

        keep_label.start()
        load_s.wait()

        @pl.loop(0, count * capacity)
        def _(slot):
            stream = index_ref[slot]
            for p in range(pairs):
                both = [held[stream, 2 * p], held[stream, 2 * p + 1]]
                outgoing[slot, p] = jnp.concatenate(both, axis=1)

        @pl.loop(1, count)
        def _(d):
            states_copy(d).start()

        keep_states.start()

    def states_wait():
        @pl.loop(1, count)
        def _(d):
            label_copy(d).wait_recv()
            states_copy(d).wait_recv()

        keep_label.wait()
        keep_states.wait()
        read_labels.start()
        read_labels.wait()

    row_block = o_hbm.shape[0]
    my_mid = 1 + me // first_half
    collects = my_mid == z

    def column_slot(source, group):
        block = source % first_half
        return obuf.at[block, pl.ds(pl.multiple_of(group * row_block, row_block), row_block)]

    column_hop = remote(o_hbm, column_slot(me, z), send_o.at[0], recv_o.at[z], (me, my_mid))
    column_own = pltpu.make_async_copy(o_hbm, column_slot(me, z), local.at[6])

    def columns_start():
        @pl.when(collects)
        def _():
            column_own.start()

        @pl.when(jnp.logical_not(collects))
        def _():
            column_hop.start()

    half_side = side // 2
    base_y = (z - 1) * half_side

    def block_copy(block, send, target):
        slot = obuf.at[block]
        return remote(slot, slot, send, recv_b.at[block], target)

    def block_of(cx, cy, c):
        return (cy - base_y) * side * 2 + cx * 2 + c

    def line_y(d):
        return block_copy(block_of(x, y, core), send_ba.at[d], (device(x, (y + d) % side), z))

    def spread_x(block, i):
        for d in range(1, side):
            block_copy(block, send_bb.at[i, d], (device((x + d) % side, y), z)).start()
        block_copy(block, send_bs.at[block], sibling).start()

    def spread_done(block, i):
        for d in range(1, side):
            block_copy(block, send_bb.at[i, d], (device((x + d) % side, y), z)).wait_send()
        block_copy(block, send_bs.at[block], sibling).wait_send()

    def columns_first():
        @pl.when(collects)
        def _():
            for d in range(1, PLANES):
                source = (z + d) % PLANES
                remote(o_hbm, column_slot(me, source), send_o.at[0], recv_o.at[source], (me, source)).wait_recv()
            column_own.wait()
            for d in range(1, side):
                line_y(d).start()
            spread_x(block_of(x, y, core), 0)

    def columns_second():
        @pl.when(is_mid)
        def _():
            for r in range(half_side):
                block = block_of(x, base_y + r, core)

                @pl.when(y != base_y + r)
                def _():
                    block_copy(block, send_ba.at[0], sibling).wait_recv()
                    spread_x(block, r + 1)

    def columns_third():
        @pl.when(is_mid)
        def _():
            for r in range(half_side):
                for d in range(1, side):
                    block = block_of((x + d) % side, base_y + r, core)
                    block_copy(block, send_ba.at[0], sibling).wait_recv()
                    block_copy(block, send_bs.at[block], sibling).start()

    def columns_last():
        @pl.when(is_mid)
        def _():
            for r in range(half_side):
                for cx in range(side):
                    block = block_of(cx, base_y + r, 1 - core)
                    block_copy(block, send_ba.at[0], sibling).wait_recv()

    def columns_done():
        @pl.when(collects)
        def _():
            for d in range(1, side):
                line_y(d).wait_send()
            spread_done(block_of(x, y, core), 0)

        @pl.when(jnp.logical_not(collects))
        def _():
            column_hop.wait_send()

        @pl.when(is_mid)
        def _():
            for r in range(half_side):

                @pl.when(y != base_y + r)
                def _():
                    spread_done(block_of(x, base_y + r, core), r + 1)

                for d in range(1, side):
                    block = block_of((x + d) % side, base_y + r, core)
                    block_copy(block, send_bs.at[block], sibling).wait_send()

    def chunk_rows(c):
        return pl.ds(pl.multiple_of(c * rows, rows), rows)

    tile = 256

    def project(c):
        @pl.loop(0, 4 * width // tile)
        def _(j):
            lanes = pl.ds(pl.multiple_of(j * tile, tile), tile)
            projected[:, lanes] = product(tok[chunk_rows(c), :], weight[:, lanes])

    length = WINDOW_LENGTH

    def attend(c, within):
        stream = c * CHUNK_STREAMS + within
        live_count = valid_ref[stream]

        def find(slot, found):
            match = places[slot // capacity, 0, slot % capacity] == stream
            return jnp.where(match, slot, found)

        where_from = lax.fori_loop(0, count * capacity, find, jnp.int32(0))
        live = (lax.broadcasted_iota(jnp.int32, (length, 1), 0) < live_count).astype(jnp.float32)
        rows_i = lax.broadcasted_iota(jnp.int32, (length, length), 0)
        cols_i = lax.broadcasted_iota(jnp.int32, (length, length), 1)
        live_row = lax.broadcasted_iota(jnp.int32, (heads, length), 1) < live_count
        lanes_at = pl.ds(pl.multiple_of(stream * length, length), length)
        decay = jnp.where(live_row, decay_ref[:, lanes_at], 0.0)
        across = lax.dot_general(
            decay,
            (rows_i <= cols_i).astype(jnp.float32),
            (((1,), (0,)), ((), ())),
            precision=lax.Precision.HIGHEST,
            preferred_element_type=jnp.float32,
        )
        down = across.T
        causal = rows_i >= cols_i
        left = lax.broadcasted_iota(jnp.int32, (length, 2 * HD), 1) < HD
        left_top = lax.broadcasted_iota(jnp.int32, (HD, 2 * HD), 1) < HD
        top = pl.ds(within * length, length)
        for p in range(pairs):
            lanes = slice(p * 2 * HD, (p + 1) * 2 * HD)

            def active(part):
                v = projected[top, part * width + lanes.start : part * width + lanes.stop]
                return v * jax.nn.sigmoid(v)

            queries = active(0).astype(jnp.bfloat16)
            keys = active(1) * live
            keys = keys.astype(jnp.bfloat16)
            values = (active(2) * live).astype(jnp.bfloat16)
            gate_in = projected[top, 3 * width + lanes.start : 3 * width + lanes.stop]
            gates = jax.nn.sigmoid(gate_in) * live
            zero = jnp.zeros_like(keys)
            key_both = jnp.concatenate([jnp.where(left, keys, zero), jnp.where(left, zero, keys)], axis=0)
            value_both = jnp.concatenate(
                [jnp.where(left, values, zero), jnp.where(left, zero, values)], axis=0
            )
            scores = product(queries, key_both, 1, 1)
            probs, alongs, lasts = [], [], []
            for sidx in range(2):
                h = 2 * p + sidx
                along, above = down[:, h : h + 1], across[h : h + 1, :]
                weights = jnp.where(causal, jnp.exp(jnp.minimum(along - above, 0.0)), 0.0)
                probs.append((scores[:, sidx * length : (sidx + 1) * length] * weights).astype(jnp.bfloat16))
                alongs.append(along)
                lasts.append(across[h : h + 1, length - 1 :])
            along = jnp.where(left, alongs[0], alongs[1])
            last = jnp.where(left[:1], lasts[0], lasts[1])
            old = incoming[where_from, p]
            block = jnp.concatenate([jnp.where(left_top, old, 0.0), jnp.where(left_top, 0.0, old)], axis=0)
            high, low = halves(block)
            carried = product(queries, high) + product(queries, low)
            attended = product(jnp.concatenate(probs, axis=1), value_both) + carried * jnp.exp(along)
            high, low = halves(keys.astype(jnp.float32) * jnp.exp(last - along))
            full = product(high, values, 0, 0) + product(low, values, 0, 0)
            fresh = jnp.exp(last) * old + jnp.where(left_top, full[:HD], full[HD:])
            updated[stream, 2 * p] = fresh[:, :HD]
            updated[stream, 2 * p + 1] = fresh[:, HD:]
            square = attended * attended
            total = jnp.sum(square, axis=1, keepdims=True)
            first = jnp.sum(jnp.where(left, square, 0.0), axis=1, keepdims=True)
            second = jnp.sum(jnp.where(left, 0.0, square), axis=1, keepdims=True)
            mean_square = jnp.where(left, first, second) * (1.0 / HD)
            result = attended * lax.rsqrt(mean_square + 1e-05) * gates
            at = pl.ds(pl.multiple_of(stream * length, length), length)
            column = pl.ds(pl.multiple_of(z * width + lanes.start, 2 * HD), 2 * HD)
            hidden[at, column] = result.astype(jnp.bfloat16)

    def hidden_slot(c, group):
        return hidden.at[chunk_rows(c), pl.ds(pl.multiple_of(group * width, width), width)]

    def hidden_own(c):
        slot = hidden_slot(c, z)
        target = jnp.where(is_mid, other_mid, 1 + half)
        return remote(slot, slot, send_h.at[c], recv_h.at[c, z], (me, target))

    def hidden_forward(c):
        slot = hidden_slot(c, outer)
        return remote(slot, slot, send_f.at[c], recv_h.at[c, outer], (me, other_mid))

    def hidden_pass(c):
        @pl.when(is_mid)
        def _():
            hidden_forward_in(c, outer).wait_recv()
            hidden_forward(c).start()

    def hidden_forward_in(c, group):
        slot = hidden_slot(c, group)
        return remote(slot, slot, send_f.at[c], recv_h.at[c, group], (me, other_mid))

    def mixed_send(c):
        part = outer - 2 * half
        src = staged.at[part, chunk_rows(c)]
        return remote(src, mixed_hbm.at[chunk_rows(c)], send_m.at[c], recv_m.at[c], (me, outer))

    def mixed_keep(c):
        part = z - 2 * half
        return pltpu.make_async_copy(
            staged.at[part, chunk_rows(c)], mixed_hbm.at[chunk_rows(c)], local_m.at[c]
        )

    def mix(c):
        @pl.when(is_mid)
        def _():
            hidden_forward_in(c, other_mid).wait_recv()
            hidden_forward_in(c, 3 - outer).wait_recv()
            at = chunk_rows(c)

            def columns_of(part):
                blocks = [product(hidden[at, :], obuf[part * per + b]) for b in range(per)]
                staged[part, at] = jnp.concatenate(blocks, axis=1).astype(jnp.bfloat16)

            @pl.loop(0, 2)
            def _(part):
                columns_of(part)

            mixed_send(c).start()
            mixed_keep(c).start()

    def states_out(c):
        at = pl.ds(c * CHUNK_STREAMS, CHUNK_STREAMS)
        return pltpu.make_async_copy(updated.at[at], updated_hbm.at[at], local_m.at[n + c])

    load_t.wait()
    send_own(0)
    load_w.wait()
    weights_start()
    send_own(1)
    columns_start()
    states_start()

    @pl.loop(0, n + 2)
    def _(i):
        @pl.when(i + 2 < n)
        def _():
            send_own(i + 2)

        @pl.when(i < n)
        def _():
            arrive(i, 1)

        @pl.when(i < 2)
        def _():
            arrive(i, 2)
            arrive(i, 3)

        @pl.when(i == 0)
        def _():
            weights_first()

        @pl.when(i == 1)
        def _():
            columns_first()
            weights_second()
            states_wait()
            weights_last()

        @pl.when((i >= 1) & (i <= n))
        def _():
            project(i - 1)

        @pl.when(i >= 2)
        def _():
            hidden_pass(i - 2)

        @pl.when((i >= 2) & (i < n))
        def _():
            arrive(i, 2)

        @pl.when(i == 2)
        def _():
            columns_second()

        @pl.when((i >= 1) & (i <= n))
        def _():
            @pl.loop(0, CHUNK_STREAMS)
            def _(within):
                @pl.when((within == CHUNK_STREAMS - 1) & (i >= 2) & (i < n))
                def _():
                    arrive(i, 3)

                attend(i - 1, within)

            hidden_own(i - 1).start()
            states_out(i - 1).start()

        @pl.when(i == 2)
        def _():
            columns_third()
            columns_last()

        @pl.when(i >= 2)
        def _():
            mix(i - 2)

    @pl.loop(0, n)
    def _(c):
        states_out(c).wait()
        hidden_own(c).wait_send()

        @pl.when(is_mid)
        def _():
            hidden_forward(c).wait_send()
            mixed_send(c).wait_send()
            mixed_keep(c).wait()

        @pl.when(is_end)
        def _():
            mixed_send(c).wait_recv()

        for f in range(PLANES):

            @pl.when((z < PLANES - 1) & (z >= f))
            def _():
                token_up(c, f).wait_send()

            @pl.when((z > 0) & (z <= f))
            def _():
                token_down(c, f).wait_send()

    columns_done()
    for d in range(1, side):
        first_copy(d).wait_send()
        second_copy(me, d, 0).wait_send()
        for e in range(1, side):
            second_copy(first_source(e), d, e).wait_send()
    for c in range(chips):
        sibling_copy(2 * c + core).wait_send()

    @pl.loop(1, count)
    def _(d):
        label_copy(d).wait_send()
        states_copy(d).wait_send()


def layer(index, valid, tokens, weight, out_weight, states, labels, log_decay):
    count, planes = lax.axis_size("stream"), lax.axis_size("tp")
    assert planes == PLANES
    chips = count // 2
    side = math.isqrt(chips)
    streams, heads = states.shape[:2]
    features = tokens.shape[1]
    total = tokens.shape[0]
    width = heads * HD
    slots = index.shape[0]
    columns = out_weight.shape[1]
    n = streams // CHUNK_STREAMS
    rows = CHUNK_STREAMS * WINDOW_LENGTH
    per = count // PLANES
    dma = pltpu.SemaphoreType.DMA
    anywhere = pl.BlockSpec(memory_space=pl.ANY)
    scalars = pl.BlockSpec(memory_space=pltpu.SMEM)
    bf16, f32 = jnp.bfloat16, jnp.float32
    return pl.pallas_call(
        functools.partial(layer_kernel, count),
        out_shape=(
            jax.ShapeDtypeStruct((total, per * columns), bf16),
            jax.ShapeDtypeStruct(states.shape, f32),
        ),
        in_specs=[scalars, scalars] + [anywhere] * 5 + [pl.BlockSpec(memory_space=pltpu.VMEM)],
        out_specs=(anywhere, anywhere),
        scratch_shapes=[
            pltpu.VMEM((total, planes * features), bf16),
            pltpu.VMEM((count * weight.shape[0], weight.shape[1]), bf16),
            pltpu.VMEM((total, planes * width), bf16),
            pltpu.VMEM((count // 2, planes * out_weight.shape[0], columns), bf16),
            pltpu.VMEM(states.shape, f32),
            pltpu.VMEM((slots, heads // 2, HD, 2 * HD), f32),
            pltpu.VMEM((slots, heads // 2, HD, 2 * HD), f32),
            pltpu.VMEM(labels.shape, jnp.int32),
            pltpu.SMEM(labels.shape, jnp.int32),
            pltpu.VMEM((rows, 4 * width), f32),
            pltpu.VMEM((2, total, per * columns), bf16),
            pltpu.VMEM(states.shape, f32),
            dma((7,)),
            dma((n, planes)),
            dma((n, planes)),
            dma((n, planes)),
            dma((count,)),
            dma((side,)),
            dma((side, side)),
            dma((count,)),
            dma((count,)),
            dma((count,)),
            dma((count,)),
            dma((count,)),
            dma((planes,)),
            dma((1,)),
            dma((count // 2,)),
            dma((side,)),
            dma((side // 2 + 1, side)),
            dma((count // 2,)),
            dma((n, planes)),
            dma((n,)),
            dma((n,)),
            dma((n,)),
            dma((n,)),
            dma((2 * n,)),
        ],
        compiler_params=pltpu.CompilerParams(
            collective_id=0, has_side_effects=True, vmem_limit_bytes=62 * 2**20
        ),
        cost_estimate=pl.CostEstimate(
            flops=30_000_000_000, bytes_accessed=60_000_000, transcendentals=0
        ),
        name="layer",
    )(index, valid, tokens, weight, out_weight, states, labels, log_decay)


def body(tokens, qkv_weight, gate_weight, out_weight, log_decay, states, dest_slot, valid):
    streams, heads = states.shape[:2]
    width = heads * HD
    count = lax.axis_size("stream")
    capacity = (streams + count - 1) // count
    order = jnp.arange(streams, dtype=jnp.int32)
    target, place = dest_slot // streams, dest_slot % streams
    earlier = (target[None, :] == target[:, None]) & (order[None, :] < order[:, None])
    rank = jnp.sum(earlier.astype(jnp.int32), axis=1)
    position = target * capacity + rank
    chosen = jnp.arange(count * capacity, dtype=jnp.int32)[:, None] == position[None, :]
    index = jnp.sum(jnp.where(chosen, order[None, :], 0), axis=1)
    label = jnp.sum(jnp.where(chosen, place[None, :] + 1, 0), axis=1) - 1
    label = jnp.pad(label.reshape(count, 1, capacity), ((0, 0), (0, 0), (0, 128 - capacity)))
    label = jnp.broadcast_to(label, (count, 8, 128))
    local = jnp.concatenate([qkv_weight.reshape(-1, 3 * width), gate_weight], axis=1)
    return layer(index, valid, tokens, local, out_weight, states, label, log_decay)


def solution(mesh):
    return jax.shard_map(
        body,
        mesh=mesh,
        in_specs=(
            P("stream", "tp"),
            P("stream", None, "tp"),
            P("stream", "tp"),
            P("tp", "stream"),
            P("tp", "stream"),
            P("stream", "tp", None, None),
            P("stream"),
            P("stream"),
        ),
        out_specs=(P("stream", "tp"), P("stream", "tp", None, None)),
        check_vma=False,
    )
```

```python
import functools
import math

import jax
import jax.numpy as jnp
from jax import lax
from jax.experimental import pallas as pl
from jax.experimental.pallas import tpu as pltpu
from jax.sharding import PartitionSpec as P

HD = 64
WINDOW_LENGTH = 128
PLANES = 4
CHUNK_STREAMS = 2
LAG = 3
MESH = pl.DeviceIdType.MESH


def remote(src, dst, send, recv, target):
    return pltpu.make_async_remote_copy(
        src_ref=src, dst_ref=dst, send_sem=send, recv_sem=recv, device_id=target, device_id_type=MESH
    )


def product(a, b, left=1, right=0):
    return lax.dot_general(a, b, (((left,), (right,)), ((), ())), preferred_element_type=jnp.float32)


def halves(x):
    high = x.astype(jnp.bfloat16)
    return high, (x - high.astype(jnp.float32)).astype(jnp.bfloat16)


def layer_kernel(
    count,
    index_ref,
    valid_ref,
    t_hbm,
    w_hbm,
    o_hbm,
    s_hbm,
    label_hbm,
    decay_ref,
    mixed_hbm,
    updated_hbm,
    tok,
    weight,
    hidden,
    obuf,
    held,
    outgoing,
    incoming,
    labels,
    places,
    projected,
    staged,
    updated,
    local,
    recv_t,
    send_up,
    send_down,
    recv_w,
    send_w1,
    send_w2,
    send_ws,
    recv_s,
    send_s,
    recv_l,
    send_l,
    recv_o,
    send_o,
    recv_b,
    send_ba,
    send_bb,
    send_bs,
    recv_h,
    send_h,
    send_f,
    recv_m,
    send_m,
    local_m,
):
    me = lax.axis_index("stream")
    z = lax.axis_index("tp")
    core, chip = me % 2, me // 2
    chips = count // 2
    side = math.isqrt(chips)
    x, y = chip % side, chip // side
    streams, heads = held.shape[:2]
    width = heads * HD
    pairs = heads // 2
    features = t_hbm.shape[1]
    depth = w_hbm.shape[0]
    capacity = outgoing.shape[0] // count
    rows = CHUNK_STREAMS * WINDOW_LENGTH
    n = streams // CHUNK_STREAMS
    per = count // PLANES
    half = z // 2
    first_half = count // 2
    is_mid = (z == 1) | (z == 2)
    is_end = (z == 0) | (z == 3)
    outer = 3 * half
    other_mid = 2 - half
    sibling = (me + 1 - 2 * core, z)

    def device(cx, cy):
        return (cy * side + cx) * 2 + core

    own_tok = tok.at[:, pl.ds(pl.multiple_of(z * features, features), features)]
    load_t = pltpu.make_async_copy(t_hbm, own_tok, local.at[0])
    load_t.start()
    own_w = weight.at[pl.ds(pl.multiple_of(me * depth, depth), depth)]
    load_w = pltpu.make_async_copy(w_hbm, own_w, local.at[1])
    load_w.start()
    load_s = pltpu.make_async_copy(s_hbm, held, local.at[2])
    load_s.start()
    barrier = pltpu.get_barrier_semaphore()

    @pl.loop(1, count)
    def _(d):
        pl.semaphore_signal(barrier, inc=1, device_id=((me + d) % count, z), device_id_type=MESH)

    for d in range(1, PLANES):
        pl.semaphore_signal(barrier, inc=1, device_id=(me, (z + d) % PLANES), device_id_type=MESH)
    pl.semaphore_wait(barrier, count - 1 + PLANES - 1)

    def token_slot(c, f):
        return tok.at[
            pl.ds(pl.multiple_of(c * rows, rows), rows),
            pl.ds(pl.multiple_of(f * features, features), features),
        ]

    def token_up(c, f):
        slot = token_slot(c, f)
        return remote(slot, slot, send_up.at[c, f], recv_t.at[c, f], (me, z + 1))

    def token_down(c, f):
        slot = token_slot(c, f)
        return remote(slot, slot, send_down.at[c, f], recv_t.at[c, f], (me, z - 1))

    def send_own(c):
        @pl.when(z < PLANES - 1)
        def _():
            token_up(c, z).start()

        @pl.when(z > 0)
        def _():
            token_down(c, z).start()

    def arrive(c, hops):
        @pl.when(z >= hops)
        def _():
            f = z - hops
            token_down(c, f).wait_recv()

            @pl.when(z < PLANES - 1)
            def _():
                token_up(c, f).start()

        @pl.when(z + hops < PLANES)
        def _():
            f = z + hops
            token_up(c, f).wait_recv()

            @pl.when(z > 0)
            def _():
                token_down(c, f).start()

    def first_peer(d):
        return ((x + d * (1 - core)) % side, (y + d * core) % side)

    def second_peer(d):
        return ((x + d * core) % side, (y + d * (1 - core)) % side)

    def weight_slot(source):
        return weight.at[pl.ds(pl.multiple_of(source * depth, depth), depth)]

    def weight_copy(source, send, target):
        slot = weight_slot(source)
        return remote(slot, slot, send, recv_w.at[source], target)

    def first_source(d):
        px, py = first_peer(-d)
        return device(px, py)

    def second_source(d, e):
        sx, sy = (x - d * core) % side, (y - d * (1 - core)) % side
        return device((sx - e * (1 - core)) % side, (sy - e * core) % side)

    def first_copy(d):
        px, py = first_peer(d)
        return weight_copy(me, send_w1.at[d], (device(px, py), z))

    def second_copy(source, d, e):
        px, py = second_peer(d)
        return weight_copy(source, send_w2.at[d, e], (device(px, py), z))

    def sibling_copy(source):
        return weight_copy(source, send_ws.at[source], sibling)

    def weights_start():
        for d in range(1, side):
            first_copy(d).start()
        for d in range(1, side):
            second_copy(me, d, 0).start()
        sibling_copy(me).start()

    def weights_first():
        for e in range(1, side):
            source = first_source(e)
            sibling_copy(source).wait_recv()
            for d in range(1, side):
                second_copy(source, d, e).start()
            sibling_copy(source).start()

    def weights_second():
        for d in range(1, side):
            for e in range(side):
                source = second_source(d, e)
                sibling_copy(source).wait_recv()
                sibling_copy(source).start()

    def weights_last():
        for c in range(chips):
            sibling_copy(2 * c + 1 - core).wait_recv()

    def slots_of(buffer, d):
        return buffer.at[pl.ds(d * capacity, capacity)]

    def states_copy(d):
        target = (me + d) % count
        return remote(
            slots_of(outgoing, target), slots_of(incoming, me), send_s.at[d], recv_s.at[d], (target, z)
        )

    def label_copy(d):
        target = (me + d) % count
        return remote(label_hbm.at[target], labels.at[me], send_l.at[d], recv_l.at[d], (target, z))

    keep_states = pltpu.make_async_copy(slots_of(outgoing, me), slots_of(incoming, me), local.at[3])
    keep_label = pltpu.make_async_copy(label_hbm.at[me], labels.at[me], local.at[4])
    read_labels = pltpu.make_async_copy(labels, places, local.at[5])

    def states_start():
        @pl.loop(1, count)
        def _(d):
            label_copy(d).start()

        keep_label.start()
        load_s.wait()

        @pl.loop(0, count * capacity)
        def _(slot):
            stream = index_ref[slot]
            for p in range(pairs):
                both = [held[stream, 2 * p], held[stream, 2 * p + 1]]
                outgoing[slot, p] = jnp.concatenate(both, axis=1)

        @pl.loop(1, count)
        def _(d):
            states_copy(d).start()

        keep_states.start()

    def states_wait():
        @pl.loop(1, count)
        def _(d):
            label_copy(d).wait_recv()
            states_copy(d).wait_recv()

        keep_label.wait()
        keep_states.wait()
        read_labels.start()
        read_labels.wait()

    row_block = o_hbm.shape[0]
    my_mid = 1 + me // first_half
    collects = my_mid == z

    def column_slot(source, group):
        block = source % first_half
        return obuf.at[block, pl.ds(pl.multiple_of(group * row_block, row_block), row_block)]

    column_hop = remote(o_hbm, column_slot(me, z), send_o.at[0], recv_o.at[z], (me, my_mid))
    column_own = pltpu.make_async_copy(o_hbm, column_slot(me, z), local.at[6])

    def columns_start():
        @pl.when(collects)
        def _():
            column_own.start()

        @pl.when(jnp.logical_not(collects))
        def _():
            column_hop.start()

    half_side = side // 2
    base_y = (z - 1) * half_side

    def piece_copy(block, group, send, target):
        slot = obuf.at[block, pl.ds(pl.multiple_of(group * row_block, row_block), row_block)]
        return remote(slot, slot, send, recv_b.at[block, group], target)

    def piece_in(block, group):
        return piece_copy(block, group, send_ba.at[group, 0], sibling)

    def block_of(cx, cy, c):
        return (cy - base_y) * side * 2 + cx * 2 + c

    def line_y(group, d):
        block = block_of(x, y, core)
        return piece_copy(block, group, send_ba.at[group, d], (device(x, (y + d) % side), z))

    def piece_x(block, group, i, d):
        return piece_copy(block, group, send_bb.at[group, i, d], (device((x + d) % side, y), z))

    def piece_sibling(block, group):
        return piece_copy(block, group, send_bs.at[block, group], sibling)

    def spread_x(block, group, i):
        for d in range(1, side):
            piece_x(block, group, i, d).start()
        piece_sibling(block, group).start()

    def spread_done(block, group, i):
        for d in range(1, side):
            piece_x(block, group, i, d).wait_send()
        piece_sibling(block, group).wait_send()

    def columns_first(d):
        @pl.when(collects)
        def _():
            source = (z + d) % PLANES
            if d == 0:
                column_own.wait()
            else:
                remote(o_hbm, column_slot(me, source), send_o.at[0], recv_o.at[source], (me, source)).wait_recv()
            for e in range(1, side):
                line_y(source, e).start()
            spread_x(block_of(x, y, core), source, 0)

    def columns_second(d):
        @pl.when(is_mid)
        def _():
            source = (z + d) % PLANES
            for r in range(half_side):

                @pl.when(y != base_y + r)
                def _():
                    block = block_of(x, base_y + r, core)
                    piece_in(block, source).wait_recv()
                    spread_x(block, source, r + 1)

    def columns_third():
        @pl.when(is_mid)
        def _():
            @pl.loop(0, PLANES)
            def _(d):
                source = (z + d) % PLANES
                for r in range(half_side):
                    for e in range(1, side):
                        block = block_of((x + e) % side, base_y + r, core)
                        piece_in(block, source).wait_recv()
                        piece_sibling(block, source).start()

    def columns_last():
        @pl.when(is_mid)
        def _():
            @pl.loop(0, PLANES)
            def _(group):
                for r in range(half_side):
                    for cx in range(side):
                        piece_in(block_of(cx, base_y + r, 1 - core), group).wait_recv()

    def columns_done():
        @pl.when(jnp.logical_not(collects))
        def _():
            column_hop.wait_send()

        @pl.loop(0, PLANES)
        def _(group):
            @pl.when(collects)
            def _():
                for d in range(1, side):
                    line_y(group, d).wait_send()
                spread_done(block_of(x, y, core), group, 0)

            @pl.when(is_mid)
            def _():
                for r in range(half_side):

                    @pl.when(y != base_y + r)
                    def _():
                        spread_done(block_of(x, base_y + r, core), group, r + 1)

                    for d in range(1, side):
                        piece_sibling(block_of((x + d) % side, base_y + r, core), group).wait_send()

    def chunk_rows(c):
        return pl.ds(pl.multiple_of(c * rows, rows), rows)

    tile = 256

    def project(c):
        @pl.loop(0, 4 * width // tile)
        def _(j):
            lanes = pl.ds(pl.multiple_of(j * tile, tile), tile)
            projected[:, lanes] = product(tok[chunk_rows(c), :], weight[:, lanes])

    length = WINDOW_LENGTH

    def attend(c, within):
        stream = c * CHUNK_STREAMS + within
        live_count = valid_ref[stream]

        def find(slot, found):
            match = places[slot // capacity, 0, slot % capacity] == stream
            return jnp.where(match, slot, found)

        where_from = lax.fori_loop(0, count * capacity, find, jnp.int32(0))
        live = (lax.broadcasted_iota(jnp.int32, (length, 1), 0) < live_count).astype(jnp.float32)
        rows_i = lax.broadcasted_iota(jnp.int32, (length, length), 0)
        cols_i = lax.broadcasted_iota(jnp.int32, (length, length), 1)
        live_row = lax.broadcasted_iota(jnp.int32, (heads, length), 1) < live_count
        lanes_at = pl.ds(pl.multiple_of(stream * length, length), length)
        decay = jnp.where(live_row, decay_ref[:, lanes_at], 0.0)
        across = lax.dot_general(
            decay,
            (rows_i <= cols_i).astype(jnp.float32),
            (((1,), (0,)), ((), ())),
            precision=lax.Precision.HIGHEST,
            preferred_element_type=jnp.float32,
        )
        down = across.T
        causal = rows_i >= cols_i
        left = lax.broadcasted_iota(jnp.int32, (length, 2 * HD), 1) < HD
        left_top = lax.broadcasted_iota(jnp.int32, (HD, 2 * HD), 1) < HD
        top = pl.ds(within * length, length)
        for p in range(pairs):
            lanes = slice(p * 2 * HD, (p + 1) * 2 * HD)

            def active(part):
                v = projected[top, part * width + lanes.start : part * width + lanes.stop]
                return v * jax.nn.sigmoid(v)

            queries = active(0).astype(jnp.bfloat16)
            keys = active(1) * live
            keys = keys.astype(jnp.bfloat16)
            values = (active(2) * live).astype(jnp.bfloat16)
            gate_in = projected[top, 3 * width + lanes.start : 3 * width + lanes.stop]
            gates = jax.nn.sigmoid(gate_in) * live
            zero = jnp.zeros_like(keys)
            key_both = jnp.concatenate([jnp.where(left, keys, zero), jnp.where(left, zero, keys)], axis=0)
            value_both = jnp.concatenate(
                [jnp.where(left, values, zero), jnp.where(left, zero, values)], axis=0
            )
            scores = product(queries, key_both, 1, 1)
            probs, alongs, lasts = [], [], []
            for sidx in range(2):
                h = 2 * p + sidx
                along, above = down[:, h : h + 1], across[h : h + 1, :]
                weights = jnp.where(causal, jnp.exp(jnp.minimum(along - above, 0.0)), 0.0)
                probs.append((scores[:, sidx * length : (sidx + 1) * length] * weights).astype(jnp.bfloat16))
                alongs.append(along)
                lasts.append(across[h : h + 1, length - 1 :])
            along = jnp.where(left, alongs[0], alongs[1])
            last = jnp.where(left[:1], lasts[0], lasts[1])
            old = incoming[where_from, p]
            block = jnp.concatenate([jnp.where(left_top, old, 0.0), jnp.where(left_top, 0.0, old)], axis=0)
            high, low = halves(block)
            carried = product(queries, high) + product(queries, low)
            attended = product(jnp.concatenate(probs, axis=1), value_both) + carried * jnp.exp(along)
            high, low = halves(keys.astype(jnp.float32) * jnp.exp(last - along))
            full = product(high, values, 0, 0) + product(low, values, 0, 0)
            fresh = jnp.exp(last) * old + jnp.where(left_top, full[:HD], full[HD:])
            updated[stream, 2 * p] = fresh[:, :HD]
            updated[stream, 2 * p + 1] = fresh[:, HD:]
            square = attended * attended
            total = jnp.sum(square, axis=1, keepdims=True)
            first = jnp.sum(jnp.where(left, square, 0.0), axis=1, keepdims=True)
            second = jnp.sum(jnp.where(left, 0.0, square), axis=1, keepdims=True)
            mean_square = jnp.where(left, first, second) * (1.0 / HD)
            result = attended * lax.rsqrt(mean_square + 1e-05) * gates
            at = pl.ds(pl.multiple_of(stream * length, length), length)
            column = pl.ds(pl.multiple_of(z * width + lanes.start, 2 * HD), 2 * HD)
            hidden[at, column] = result.astype(jnp.bfloat16)

    def hidden_slot(c, group):
        return hidden.at[chunk_rows(c), pl.ds(pl.multiple_of(group * width, width), width)]

    def hidden_own(c):
        slot = hidden_slot(c, z)
        target = jnp.where(is_mid, other_mid, 1 + half)
        return remote(slot, slot, send_h.at[c], recv_h.at[c, z], (me, target))

    def hidden_forward(c):
        slot = hidden_slot(c, outer)
        return remote(slot, slot, send_f.at[c], recv_h.at[c, outer], (me, other_mid))

    def hidden_pass(c):
        @pl.when(is_mid)
        def _():
            hidden_forward_in(c, outer).wait_recv()
            hidden_forward(c).start()

    def hidden_forward_in(c, group):
        slot = hidden_slot(c, group)
        return remote(slot, slot, send_f.at[c], recv_h.at[c, group], (me, other_mid))

    def mixed_send(c):
        part = outer - 2 * half
        src = staged.at[part, chunk_rows(c)]
        return remote(src, mixed_hbm.at[chunk_rows(c)], send_m.at[c], recv_m.at[c], (me, outer))

    def mixed_keep(c):
        part = z - 2 * half
        return pltpu.make_async_copy(
            staged.at[part, chunk_rows(c)], mixed_hbm.at[chunk_rows(c)], local_m.at[c]
        )

    def mix(c):
        @pl.when(is_mid)
        def _():
            hidden_forward_in(c, other_mid).wait_recv()
            hidden_forward_in(c, 3 - outer).wait_recv()
            at = chunk_rows(c)

            def columns_of(part):
                blocks = [product(hidden[at, :], obuf[part * per + b]) for b in range(per)]
                staged[part, at] = jnp.concatenate(blocks, axis=1).astype(jnp.bfloat16)

            @pl.loop(0, 2)
            def _(part):
                columns_of(part)

            mixed_send(c).start()
            mixed_keep(c).start()

    def states_out(c):
        at = pl.ds(c * CHUNK_STREAMS, CHUNK_STREAMS)
        return pltpu.make_async_copy(updated.at[at], updated_hbm.at[at], local_m.at[n + c])

    load_t.wait()
    send_own(0)
    load_w.wait()
    weights_start()

    @pl.when(is_end)
    def _():
        @pl.loop(1, n)
        def _(c):
            send_own(c)

        columns_start()

    states_start()
    shift = jnp.where(is_mid, 1, 0)

    @pl.loop(0, n + LAG)
    def _(i):
        k = i - LAG

        @pl.when(is_mid & (i < n))
        def _():
            arrive(i, 1)

            @pl.when(i + 1 < n)
            def _():
                send_own(i + 1)

        @pl.when(is_mid & (i < LAG))
        def _():
            arrive(i, 2)

        @pl.when(is_mid & (i == 1))
        def _():
            columns_start()
            columns_first(0)

        @pl.when(i == shift)
        def _():
            weights_first()

        @pl.when(i == 1 + shift)
        def _():
            weights_second()

        @pl.when(i == LAG)
        def _():
            weights_last()

        @pl.when(k >= 0)
        def _():
            @pl.when(is_end)
            def _():
                arrive(k, 1)
                arrive(k, 2)
                arrive(k, 3)

            project(k)

        @pl.when(is_mid & (k >= 0) & (i < n))
        def _():
            arrive(i, 2)

        @pl.when(k >= LAG)
        def _():
            hidden_pass(k - LAG)

        @pl.when(k == 0)
        def _():
            states_wait()
            for d in range(1, PLANES):
                columns_first(d)

        @pl.when(k >= 0)
        def _():
            @pl.loop(0, CHUNK_STREAMS)
            def _(within):
                attend(k, within)

            hidden_own(k).start()
            states_out(k).start()

        for d in range(PLANES):

            @pl.when(k == 1 + d)
            def _():
                columns_second(d)

    hidden_pass(n - LAG)
    columns_third()
    columns_last()

    @pl.loop(0, n)
    def _(c):
        @pl.when(c == n - 4)
        def _():
            hidden_pass(n - 2)

        @pl.when(c == n - 1)
        def _():
            hidden_pass(n - 1)

        mix(c)

    @pl.loop(0, n)
    def _(c):
        states_out(c).wait()
        hidden_own(c).wait_send()

        @pl.when(is_mid)
        def _():
            hidden_forward(c).wait_send()
            mixed_send(c).wait_send()
            mixed_keep(c).wait()

        @pl.when(is_end)
        def _():
            mixed_send(c).wait_recv()

        for f in range(PLANES):

            @pl.when((z < PLANES - 1) & (z >= f))
            def _():
                token_up(c, f).wait_send()

            @pl.when((z > 0) & (z <= f))
            def _():
                token_down(c, f).wait_send()

    columns_done()
    for d in range(1, side):
        first_copy(d).wait_send()
        second_copy(me, d, 0).wait_send()
        for e in range(1, side):
            second_copy(first_source(e), d, e).wait_send()
    for c in range(chips):
        sibling_copy(2 * c + core).wait_send()

    @pl.loop(1, count)
    def _(d):
        label_copy(d).wait_send()
        states_copy(d).wait_send()


def layer(index, valid, tokens, weight, out_weight, states, labels, log_decay):
    count, planes = lax.axis_size("stream"), lax.axis_size("tp")
    assert planes == PLANES
    chips = count // 2
    side = math.isqrt(chips)
    streams, heads = states.shape[:2]
    features = tokens.shape[1]
    total = tokens.shape[0]
    width = heads * HD
    slots = index.shape[0]
    columns = out_weight.shape[1]
    n = streams // CHUNK_STREAMS
    rows = CHUNK_STREAMS * WINDOW_LENGTH
    per = count // PLANES
    dma = pltpu.SemaphoreType.DMA
    anywhere = pl.BlockSpec(memory_space=pl.ANY)
    scalars = pl.BlockSpec(memory_space=pltpu.SMEM)
    bf16, f32 = jnp.bfloat16, jnp.float32
    return pl.pallas_call(
        functools.partial(layer_kernel, count),
        out_shape=(
            jax.ShapeDtypeStruct((total, per * columns), bf16),
            jax.ShapeDtypeStruct(states.shape, f32),
        ),
        in_specs=[scalars, scalars] + [anywhere] * 5 + [pl.BlockSpec(memory_space=pltpu.VMEM)],
        out_specs=(anywhere, anywhere),
        scratch_shapes=[
            pltpu.VMEM((total, planes * features), bf16),
            pltpu.VMEM((count * weight.shape[0], weight.shape[1]), bf16),
            pltpu.VMEM((total, planes * width), bf16),
            pltpu.VMEM((count // 2, planes * out_weight.shape[0], columns), bf16),
            pltpu.VMEM(states.shape, f32),
            pltpu.VMEM((slots, heads // 2, HD, 2 * HD), f32),
            pltpu.VMEM((slots, heads // 2, HD, 2 * HD), f32),
            pltpu.VMEM(labels.shape, jnp.int32),
            pltpu.SMEM(labels.shape, jnp.int32),
            pltpu.VMEM((rows, 4 * width), f32),
            pltpu.VMEM((2, total, per * columns), bf16),
            pltpu.VMEM(states.shape, f32),
            dma((7,)),
            dma((n, planes)),
            dma((n, planes)),
            dma((n, planes)),
            dma((count,)),
            dma((side,)),
            dma((side, side)),
            dma((count,)),
            dma((count,)),
            dma((count,)),
            dma((count,)),
            dma((count,)),
            dma((planes,)),
            dma((1,)),
            dma((count // 2, planes)),
            dma((planes, side)),
            dma((planes, side // 2 + 1, side)),
            dma((count // 2, planes)),
            dma((n, planes)),
            dma((n,)),
            dma((n,)),
            dma((n,)),
            dma((n,)),
            dma((2 * n,)),
        ],
        compiler_params=pltpu.CompilerParams(
            collective_id=0, has_side_effects=True, vmem_limit_bytes=62 * 2**20
        ),
        cost_estimate=pl.CostEstimate(
            flops=30_000_000_000, bytes_accessed=60_000_000, transcendentals=0
        ),
        name="layer",
    )(index, valid, tokens, weight, out_weight, states, labels, log_decay)


def body(tokens, qkv_weight, gate_weight, out_weight, log_decay, states, dest_slot, valid):
    streams, heads = states.shape[:2]
    width = heads * HD
    count = lax.axis_size("stream")
    capacity = (streams + count - 1) // count
    order = jnp.arange(streams, dtype=jnp.int32)
    target, place = dest_slot // streams, dest_slot % streams
    earlier = (target[None, :] == target[:, None]) & (order[None, :] < order[:, None])
    rank = jnp.sum(earlier.astype(jnp.int32), axis=1)
    position = target * capacity + rank
    chosen = jnp.arange(count * capacity, dtype=jnp.int32)[:, None] == position[None, :]
    index = jnp.sum(jnp.where(chosen, order[None, :], 0), axis=1)
    label = jnp.sum(jnp.where(chosen, place[None, :] + 1, 0), axis=1) - 1
    label = jnp.pad(label.reshape(count, 1, capacity), ((0, 0), (0, 0), (0, 128 - capacity)))
    label = jnp.broadcast_to(label, (count, 8, 128))
    local = jnp.concatenate([qkv_weight.reshape(-1, 3 * width), gate_weight], axis=1)
    return layer(index, valid, tokens, local, out_weight, states, label, log_decay)


def solution(mesh):
    return jax.shard_map(
        body,
        mesh=mesh,
        in_specs=(
            P("stream", "tp"),
            P("stream", None, "tp"),
            P("stream", "tp"),
            P("tp", "stream"),
            P("tp", "stream"),
            P("stream", "tp", None, None),
            P("stream"),
            P("stream"),
        ),
        out_specs=(P("stream", "tp"), P("stream", "tp", None, None)),
        check_vma=False,
    )
```

```python
import functools
import math

import jax
import jax.numpy as jnp
from jax import lax
from jax.experimental import pallas as pl
from jax.experimental.pallas import tpu as pltpu
from jax.sharding import PartitionSpec as P

HD = 64
WINDOW_LENGTH = 128
PLANES = 4
CHUNK_STREAMS = 2
LAG = 3
MESH = pl.DeviceIdType.MESH


def remote(src, dst, send, recv, target):
    return pltpu.make_async_remote_copy(
        src_ref=src, dst_ref=dst, send_sem=send, recv_sem=recv, device_id=target, device_id_type=MESH
    )


def product(a, b, left=1, right=0):
    return lax.dot_general(a, b, (((left,), (right,)), ((), ())), preferred_element_type=jnp.float32)


def halves(x):
    high = x.astype(jnp.bfloat16)
    return high, (x - high.astype(jnp.float32)).astype(jnp.bfloat16)


def layer_kernel(
    count,
    index_ref,
    valid_ref,
    t_hbm,
    w_hbm,
    g_hbm,
    o_hbm,
    s_hbm,
    label_hbm,
    decay_ref,
    mixed_hbm,
    updated_hbm,
    tok,
    weight,
    hidden,
    obuf,
    held,
    outgoing,
    incoming,
    labels,
    places,
    projected,
    staged,
    updated,
    local,
    recv_t,
    send_up,
    send_down,
    recv_w,
    send_w1,
    send_w2,
    send_ws,
    recv_s,
    send_s,
    recv_l,
    send_l,
    recv_o,
    send_o,
    recv_b,
    send_ba,
    send_bb,
    send_bs,
    recv_h,
    send_h,
    send_f,
    recv_m,
    send_m,
    local_m,
):
    me = lax.axis_index("stream")
    z = lax.axis_index("tp")
    core, chip = me % 2, me // 2
    chips = count // 2
    side = math.isqrt(chips)
    x, y = chip % side, chip // side
    streams, heads = held.shape[:2]
    width = heads * HD
    pairs = heads // 2
    features = t_hbm.shape[1]
    depth = g_hbm.shape[0]
    capacity = outgoing.shape[0] // count
    rows = CHUNK_STREAMS * WINDOW_LENGTH
    n = streams // CHUNK_STREAMS
    per = count // PLANES
    half = z // 2
    first_half = count // 2
    is_mid = (z == 1) | (z == 2)
    is_end = (z == 0) | (z == 3)
    outer = 3 * half
    other_mid = 2 - half
    sibling = (me + 1 - 2 * core, z)

    def device(cx, cy):
        return (cy * side + cx) * 2 + core

    own_tok = tok.at[:, pl.ds(pl.multiple_of(z * features, features), features)]
    load_t = pltpu.make_async_copy(t_hbm, own_tok, local.at[0])
    load_t.start()

    def load_w(part):
        source = g_hbm if part == 3 else w_hbm.at[part]
        at = (pl.ds(pl.multiple_of(me * depth, depth), depth), pl.ds(part * width, width))
        return pltpu.make_async_copy(source, weight.at[at], local.at[7 + part])

    for part in range(4):
        load_w(part).start()
    load_s = pltpu.make_async_copy(s_hbm, held, local.at[2])
    load_s.start()
    barrier = pltpu.get_barrier_semaphore()

    @pl.loop(1, count)
    def _(d):
        pl.semaphore_signal(barrier, inc=1, device_id=((me + d) % count, z), device_id_type=MESH)

    for d in range(1, PLANES):
        pl.semaphore_signal(barrier, inc=1, device_id=(me, (z + d) % PLANES), device_id_type=MESH)
    pl.semaphore_wait(barrier, count - 1 + PLANES - 1)

    def token_slot(c, f):
        return tok.at[
            pl.ds(pl.multiple_of(c * rows, rows), rows),
            pl.ds(pl.multiple_of(f * features, features), features),
        ]

    def token_up(c, f):
        slot = token_slot(c, f)
        return remote(slot, slot, send_up.at[c, f], recv_t.at[c, f], (me, z + 1))

    def token_down(c, f):
        slot = token_slot(c, f)
        return remote(slot, slot, send_down.at[c, f], recv_t.at[c, f], (me, z - 1))

    def send_own(c):
        @pl.when(z < PLANES - 1)
        def _():
            token_up(c, z).start()

        @pl.when(z > 0)
        def _():
            token_down(c, z).start()

    def arrive(c, hops):
        @pl.when(z >= hops)
        def _():
            f = z - hops
            token_down(c, f).wait_recv()

            @pl.when(z < PLANES - 1)
            def _():
                token_up(c, f).start()

        @pl.when(z + hops < PLANES)
        def _():
            f = z + hops
            token_up(c, f).wait_recv()

            @pl.when(z > 0)
            def _():
                token_down(c, f).start()

    def first_peer(d):
        return ((x + d * (1 - core)) % side, (y + d * core) % side)

    def second_peer(d):
        return ((x + d * core) % side, (y + d * (1 - core)) % side)

    def weight_slot(source):
        return weight.at[pl.ds(pl.multiple_of(source * depth, depth), depth)]

    def weight_copy(source, send, target):
        slot = weight_slot(source)
        return remote(slot, slot, send, recv_w.at[source], target)

    def first_source(d):
        px, py = first_peer(-d)
        return device(px, py)

    def second_source(d, e):
        sx, sy = (x - d * core) % side, (y - d * (1 - core)) % side
        return device((sx - e * (1 - core)) % side, (sy - e * core) % side)

    def first_copy(d):
        px, py = first_peer(d)
        return weight_copy(me, send_w1.at[d], (device(px, py), z))

    def second_copy(source, d, e):
        px, py = second_peer(d)
        return weight_copy(source, send_w2.at[d, e], (device(px, py), z))

    def sibling_copy(source):
        return weight_copy(source, send_ws.at[source], sibling)

    def weights_start():
        for d in range(1, side):
            first_copy(d).start()
        for d in range(1, side):
            second_copy(me, d, 0).start()
        sibling_copy(me).start()

    def weights_first():
        for e in range(1, side):
            source = first_source(e)
            sibling_copy(source).wait_recv()
            for d in range(1, side):
                second_copy(source, d, e).start()
            sibling_copy(source).start()

    def weights_second():
        for d in range(1, side):
            for e in range(side):
                source = second_source(d, e)
                sibling_copy(source).wait_recv()
                sibling_copy(source).start()

    def weights_last():
        for c in range(chips):
            sibling_copy(2 * c + 1 - core).wait_recv()

    def slots_of(buffer, d):
        return buffer.at[pl.ds(d * capacity, capacity)]

    def states_copy(d):
        target = (me + d) % count
        return remote(
            slots_of(outgoing, target), slots_of(incoming, me), send_s.at[d], recv_s.at[d], (target, z)
        )

    def label_copy(d):
        target = (me + d) % count
        return remote(label_hbm.at[target], labels.at[me], send_l.at[d], recv_l.at[d], (target, z))

    keep_states = pltpu.make_async_copy(slots_of(outgoing, me), slots_of(incoming, me), local.at[3])
    keep_label = pltpu.make_async_copy(label_hbm.at[me], labels.at[me], local.at[4])
    read_labels = pltpu.make_async_copy(labels, places, local.at[5])

    def states_start():
        @pl.loop(1, count)
        def _(d):
            label_copy(d).start()

        keep_label.start()
        load_s.wait()

        @pl.loop(0, count * capacity)
        def _(slot):
            stream = index_ref[slot]
            for p in range(pairs):
                both = [held[stream, 2 * p], held[stream, 2 * p + 1]]
                outgoing[slot, p] = jnp.concatenate(both, axis=1)

        @pl.loop(1, count)
        def _(d):
            states_copy(d).start()

        keep_states.start()

    def states_wait():
        @pl.loop(1, count)
        def _(d):
            label_copy(d).wait_recv()
            states_copy(d).wait_recv()

        keep_label.wait()
        keep_states.wait()
        read_labels.start()
        read_labels.wait()

    row_block = o_hbm.shape[0]
    my_mid = 1 + me // first_half
    collects = my_mid == z

    def column_slot(source, group):
        block = source % first_half
        return obuf.at[block, pl.ds(pl.multiple_of(group * row_block, row_block), row_block)]

    column_hop = remote(o_hbm, column_slot(me, z), send_o.at[0], recv_o.at[z], (me, my_mid))
    column_own = pltpu.make_async_copy(o_hbm, column_slot(me, z), local.at[6])

    def columns_start():
        @pl.when(collects)
        def _():
            column_own.start()

        @pl.when(jnp.logical_not(collects))
        def _():
            column_hop.start()

    half_side = side // 2
    base_y = (z - 1) * half_side

    def piece_copy(block, group, send, target):
        slot = obuf.at[block, pl.ds(pl.multiple_of(group * row_block, row_block), row_block)]
        return remote(slot, slot, send, recv_b.at[block, group], target)

    def piece_in(block, group):
        return piece_copy(block, group, send_ba.at[group, 0], sibling)

    def block_of(cx, cy, c):
        return (cy - base_y) * side * 2 + cx * 2 + c

    def line_y(group, d):
        block = block_of(x, y, core)
        return piece_copy(block, group, send_ba.at[group, d], (device(x, (y + d) % side), z))

    def piece_x(block, group, i, d):
        return piece_copy(block, group, send_bb.at[group, i, d], (device((x + d) % side, y), z))

    def piece_sibling(block, group):
        return piece_copy(block, group, send_bs.at[block, group], sibling)

    def spread_x(block, group, i):
        for d in range(1, side):
            piece_x(block, group, i, d).start()
        piece_sibling(block, group).start()

    def spread_done(block, group, i):
        for d in range(1, side):
            piece_x(block, group, i, d).wait_send()
        piece_sibling(block, group).wait_send()

    def columns_first(d):
        @pl.when(collects)
        def _():
            source = (z + d) % PLANES
            if d == 0:
                column_own.wait()
            else:
                remote(o_hbm, column_slot(me, source), send_o.at[0], recv_o.at[source], (me, source)).wait_recv()
            for e in range(1, side):
                line_y(source, e).start()
            spread_x(block_of(x, y, core), source, 0)

    def columns_second(d):
        @pl.when(is_mid)
        def _():
            source = (z + d) % PLANES
            for r in range(half_side):

                @pl.when(y != base_y + r)
                def _():
                    block = block_of(x, base_y + r, core)
                    piece_in(block, source).wait_recv()
                    spread_x(block, source, r + 1)

    def columns_third():
        @pl.when(is_mid)
        def _():
            @pl.loop(0, PLANES)
            def _(d):
                source = (z + d) % PLANES
                for r in range(half_side):
                    for e in range(1, side):
                        block = block_of((x + e) % side, base_y + r, core)
                        piece_in(block, source).wait_recv()
                        piece_sibling(block, source).start()

    def columns_last():
        @pl.when(is_mid)
        def _():
            @pl.loop(0, PLANES)
            def _(group):
                for r in range(half_side):
                    for cx in range(side):
                        piece_in(block_of(cx, base_y + r, 1 - core), group).wait_recv()

    def columns_done():
        @pl.when(jnp.logical_not(collects))
        def _():
            column_hop.wait_send()

        @pl.loop(0, PLANES)
        def _(group):
            @pl.when(collects)
            def _():
                for d in range(1, side):
                    line_y(group, d).wait_send()
                spread_done(block_of(x, y, core), group, 0)

            @pl.when(is_mid)
            def _():
                for r in range(half_side):

                    @pl.when(y != base_y + r)
                    def _():
                        spread_done(block_of(x, base_y + r, core), group, r + 1)

                    for d in range(1, side):
                        piece_sibling(block_of((x + d) % side, base_y + r, core), group).wait_send()

    def chunk_rows(c):
        return pl.ds(pl.multiple_of(c * rows, rows), rows)

    tile = 256

    def project(c):
        @pl.loop(0, 4 * width // tile)
        def _(j):
            lanes = pl.ds(pl.multiple_of(j * tile, tile), tile)
            projected[:, lanes] = product(tok[chunk_rows(c), :], weight[:, lanes])

    length = WINDOW_LENGTH

    def attend(c, within):
        stream = c * CHUNK_STREAMS + within
        live_count = valid_ref[stream]

        def find(slot, found):
            match = places[slot // capacity, 0, slot % capacity] == stream
            return jnp.where(match, slot, found)

        where_from = lax.fori_loop(0, count * capacity, find, jnp.int32(0))
        live = (lax.broadcasted_iota(jnp.int32, (length, 1), 0) < live_count).astype(jnp.float32)
        rows_i = lax.broadcasted_iota(jnp.int32, (length, length), 0)
        cols_i = lax.broadcasted_iota(jnp.int32, (length, length), 1)
        live_row = lax.broadcasted_iota(jnp.int32, (heads, length), 1) < live_count
        lanes_at = pl.ds(pl.multiple_of(stream * length, length), length)
        decay = jnp.where(live_row, decay_ref[:, lanes_at], 0.0)
        across = lax.dot_general(
            decay,
            (rows_i <= cols_i).astype(jnp.float32),
            (((1,), (0,)), ((), ())),
            precision=lax.Precision.HIGHEST,
            preferred_element_type=jnp.float32,
        )
        down = across.T
        causal = rows_i >= cols_i
        left = lax.broadcasted_iota(jnp.int32, (length, 2 * HD), 1) < HD
        left_top = lax.broadcasted_iota(jnp.int32, (HD, 2 * HD), 1) < HD
        top = pl.ds(within * length, length)
        for p in range(pairs):
            lanes = slice(p * 2 * HD, (p + 1) * 2 * HD)

            def active(part):
                v = projected[top, part * width + lanes.start : part * width + lanes.stop]
                return v * jax.nn.sigmoid(v)

            queries = active(0).astype(jnp.bfloat16)
            keys = active(1) * live
            keys = keys.astype(jnp.bfloat16)
            values = (active(2) * live).astype(jnp.bfloat16)
            gate_in = projected[top, 3 * width + lanes.start : 3 * width + lanes.stop]
            gates = jax.nn.sigmoid(gate_in) * live
            zero = jnp.zeros_like(keys)
            key_both = jnp.concatenate([jnp.where(left, keys, zero), jnp.where(left, zero, keys)], axis=0)
            value_both = jnp.concatenate(
                [jnp.where(left, values, zero), jnp.where(left, zero, values)], axis=0
            )
            scores = product(queries, key_both, 1, 1)
            probs, alongs, lasts = [], [], []
            for sidx in range(2):
                h = 2 * p + sidx
                along, above = down[:, h : h + 1], across[h : h + 1, :]
                weights = jnp.where(causal, jnp.exp(jnp.minimum(along - above, 0.0)), 0.0)
                probs.append((scores[:, sidx * length : (sidx + 1) * length] * weights).astype(jnp.bfloat16))
                alongs.append(along)
                lasts.append(across[h : h + 1, length - 1 :])
            along = jnp.where(left, alongs[0], alongs[1])
            last = jnp.where(left[:1], lasts[0], lasts[1])
            old = incoming[where_from, p]
            block = jnp.concatenate([jnp.where(left_top, old, 0.0), jnp.where(left_top, 0.0, old)], axis=0)
            high, low = halves(block)
            carried = product(queries, high) + product(queries, low)
            attended = product(jnp.concatenate(probs, axis=1), value_both) + carried * jnp.exp(along)
            high, low = halves(keys.astype(jnp.float32) * jnp.exp(last - along))
            full = product(high, values, 0, 0) + product(low, values, 0, 0)
            fresh = jnp.exp(last) * old + jnp.where(left_top, full[:HD], full[HD:])
            updated[stream, 2 * p] = fresh[:, :HD]
            updated[stream, 2 * p + 1] = fresh[:, HD:]
            square = attended * attended
            total = jnp.sum(square, axis=1, keepdims=True)
            first = jnp.sum(jnp.where(left, square, 0.0), axis=1, keepdims=True)
            second = jnp.sum(jnp.where(left, 0.0, square), axis=1, keepdims=True)
            mean_square = jnp.where(left, first, second) * (1.0 / HD)
            result = attended * lax.rsqrt(mean_square + 1e-05) * gates
            at = pl.ds(pl.multiple_of(stream * length, length), length)
            column = pl.ds(pl.multiple_of(z * width + lanes.start, 2 * HD), 2 * HD)
            hidden[at, column] = result.astype(jnp.bfloat16)

    def hidden_slot(c, group):
        return hidden.at[chunk_rows(c), pl.ds(pl.multiple_of(group * width, width), width)]

    def hidden_own(c):
        slot = hidden_slot(c, z)
        target = jnp.where(is_mid, other_mid, 1 + half)
        return remote(slot, slot, send_h.at[c], recv_h.at[c, z], (me, target))

    def hidden_forward(c):
        slot = hidden_slot(c, outer)
        return remote(slot, slot, send_f.at[c], recv_h.at[c, outer], (me, other_mid))

    def hidden_pass(c):
        @pl.when(is_mid)
        def _():
            hidden_forward_in(c, outer).wait_recv()
            hidden_forward(c).start()

    def hidden_forward_in(c, group):
        slot = hidden_slot(c, group)
        return remote(slot, slot, send_f.at[c], recv_h.at[c, group], (me, other_mid))

    def mixed_send(c):
        part = outer - 2 * half
        src = staged.at[part, chunk_rows(c)]
        return remote(src, mixed_hbm.at[chunk_rows(c)], send_m.at[c], recv_m.at[c], (me, outer))

    def mixed_keep(c):
        part = z - 2 * half
        return pltpu.make_async_copy(
            staged.at[part, chunk_rows(c)], mixed_hbm.at[chunk_rows(c)], local_m.at[c]
        )

    def mix(c):
        @pl.when(is_mid)
        def _():
            hidden_forward_in(c, other_mid).wait_recv()
            hidden_forward_in(c, 3 - outer).wait_recv()
            at = chunk_rows(c)

            def columns_of(part):
                blocks = [product(hidden[at, :], obuf[part * per + b]) for b in range(per)]
                staged[part, at] = jnp.concatenate(blocks, axis=1).astype(jnp.bfloat16)

            @pl.loop(0, 2)
            def _(part):
                columns_of(part)

            mixed_send(c).start()
            mixed_keep(c).start()

    def states_out(c):
        at = pl.ds(c * CHUNK_STREAMS, CHUNK_STREAMS)
        return pltpu.make_async_copy(updated.at[at], updated_hbm.at[at], local_m.at[n + c])

    load_t.wait()
    send_own(0)
    for part in range(4):
        load_w(part).wait()
    weights_start()

    @pl.when(is_end)
    def _():
        @pl.loop(1, n)
        def _(c):
            send_own(c)

        columns_start()

    states_start()
    shift = jnp.where(is_mid, 1, 0)

    @pl.loop(0, n + LAG)
    def _(i):
        k = i - LAG

        @pl.when(is_mid & (i < n))
        def _():
            arrive(i, 1)

            @pl.when(i + 1 < n)
            def _():
                send_own(i + 1)

        @pl.when(is_mid & (i < LAG))
        def _():
            arrive(i, 2)

        @pl.when(is_mid & (i == 1))
        def _():
            columns_start()
            columns_first(0)

        @pl.when(i == shift)
        def _():
            weights_first()

        @pl.when(i == 1 + shift)
        def _():
            weights_second()

        @pl.when(i == LAG)
        def _():
            weights_last()

        @pl.when(k >= 0)
        def _():
            @pl.when(is_end)
            def _():
                arrive(k, 1)
                arrive(k, 2)
                arrive(k, 3)

            project(k)

        @pl.when(is_mid & (k >= 0) & (i < n))
        def _():
            arrive(i, 2)

        @pl.when(k >= LAG)
        def _():
            hidden_pass(k - LAG)

        @pl.when(k == 0)
        def _():
            states_wait()
            for d in range(1, PLANES):
                columns_first(d)

        @pl.when(k >= 0)
        def _():
            @pl.loop(0, CHUNK_STREAMS)
            def _(within):
                attend(k, within)

            hidden_own(k).start()
            states_out(k).start()

        for d in range(PLANES):

            @pl.when(k == 1 + d)
            def _():
                columns_second(d)

    hidden_pass(n - LAG)
    columns_third()
    columns_last()

    @pl.loop(0, n)
    def _(c):
        @pl.when(c == n - 4)
        def _():
            hidden_pass(n - 2)

        @pl.when(c == n - 1)
        def _():
            hidden_pass(n - 1)

        mix(c)

    @pl.loop(0, n)
    def _(c):
        states_out(c).wait()
        hidden_own(c).wait_send()

        @pl.when(is_mid)
        def _():
            hidden_forward(c).wait_send()
            mixed_send(c).wait_send()
            mixed_keep(c).wait()

        @pl.when(is_end)
        def _():
            mixed_send(c).wait_recv()

        for f in range(PLANES):

            @pl.when((z < PLANES - 1) & (z >= f))
            def _():
                token_up(c, f).wait_send()

            @pl.when((z > 0) & (z <= f))
            def _():
                token_down(c, f).wait_send()

    columns_done()
    for d in range(1, side):
        first_copy(d).wait_send()
        second_copy(me, d, 0).wait_send()
        for e in range(1, side):
            second_copy(first_source(e), d, e).wait_send()
    for c in range(chips):
        sibling_copy(2 * c + core).wait_send()

    @pl.loop(1, count)
    def _(d):
        label_copy(d).wait_send()
        states_copy(d).wait_send()


def layer(index, valid, tokens, weight, gate_weight, out_weight, states, labels, log_decay):
    count, planes = lax.axis_size("stream"), lax.axis_size("tp")
    assert planes == PLANES
    chips = count // 2
    side = math.isqrt(chips)
    streams, heads = states.shape[:2]
    features = tokens.shape[1]
    total = tokens.shape[0]
    width = heads * HD
    slots = index.shape[0]
    columns = out_weight.shape[1]
    n = streams // CHUNK_STREAMS
    rows = CHUNK_STREAMS * WINDOW_LENGTH
    per = count // PLANES
    dma = pltpu.SemaphoreType.DMA
    anywhere = pl.BlockSpec(memory_space=pl.ANY)
    scalars = pl.BlockSpec(memory_space=pltpu.SMEM)
    bf16, f32 = jnp.bfloat16, jnp.float32
    return pl.pallas_call(
        functools.partial(layer_kernel, count),
        out_shape=(
            jax.ShapeDtypeStruct((total, per * columns), bf16),
            jax.ShapeDtypeStruct(states.shape, f32),
        ),
        in_specs=[scalars, scalars] + [anywhere] * 6 + [pl.BlockSpec(memory_space=pltpu.VMEM)],
        out_specs=(anywhere, anywhere),
        scratch_shapes=[
            pltpu.VMEM((total, planes * features), bf16),
            pltpu.VMEM((count * gate_weight.shape[0], 4 * width), bf16),
            pltpu.VMEM((total, planes * width), bf16),
            pltpu.VMEM((count // 2, planes * out_weight.shape[0], columns), bf16),
            pltpu.VMEM(states.shape, f32),
            pltpu.VMEM((slots, heads // 2, HD, 2 * HD), f32),
            pltpu.VMEM((slots, heads // 2, HD, 2 * HD), f32),
            pltpu.VMEM(labels.shape, jnp.int32),
            pltpu.SMEM(labels.shape, jnp.int32),
            pltpu.VMEM((rows, 4 * width), f32),
            pltpu.VMEM((2, total, per * columns), bf16),
            pltpu.VMEM(states.shape, f32),
            dma((11,)),
            dma((n, planes)),
            dma((n, planes)),
            dma((n, planes)),
            dma((count,)),
            dma((side,)),
            dma((side, side)),
            dma((count,)),
            dma((count,)),
            dma((count,)),
            dma((count,)),
            dma((count,)),
            dma((planes,)),
            dma((1,)),
            dma((count // 2, planes)),
            dma((planes, side)),
            dma((planes, side // 2 + 1, side)),
            dma((count // 2, planes)),
            dma((n, planes)),
            dma((n,)),
            dma((n,)),
            dma((n,)),
            dma((n,)),
            dma((2 * n,)),
        ],
        compiler_params=pltpu.CompilerParams(
            collective_id=0, has_side_effects=True, vmem_limit_bytes=62 * 2**20
        ),
        cost_estimate=pl.CostEstimate(
            flops=30_000_000_000, bytes_accessed=60_000_000, transcendentals=0
        ),
        name="layer",
    )(index, valid, tokens, weight, gate_weight, out_weight, states, labels, log_decay)


def body(tokens, qkv_weight, gate_weight, out_weight, log_decay, states, dest_slot, valid):
    streams = states.shape[0]
    count = lax.axis_size("stream")
    capacity = (streams + count - 1) // count
    order = jnp.arange(streams, dtype=jnp.int32)
    target, place = dest_slot // streams, dest_slot % streams
    earlier = (target[None, :] == target[:, None]) & (order[None, :] < order[:, None])
    rank = jnp.sum(earlier.astype(jnp.int32), axis=1)
    position = target * capacity + rank
    chosen = jnp.arange(count * capacity, dtype=jnp.int32)[:, None] == position[None, :]
    index = jnp.sum(jnp.where(chosen, order[None, :], 0), axis=1)
    label = jnp.sum(jnp.where(chosen, place[None, :] + 1, 0), axis=1) - 1
    label = jnp.pad(label.reshape(count, 1, capacity), ((0, 0), (0, 0), (0, 128 - capacity)))
    label = jnp.broadcast_to(label, (count, 8, 128))
    local = qkv_weight.transpose(1, 0, 2)
    return layer(index, valid, tokens, local, gate_weight, out_weight, states, label, log_decay)


def solution(mesh):
    return jax.shard_map(
        body,
        mesh=mesh,
        in_specs=(
            P("stream", "tp"),
            P("stream", None, "tp"),
            P("stream", "tp"),
            P("tp", "stream"),
            P("tp", "stream"),
            P("stream", "tp", None, None),
            P("stream"),
            P("stream"),
        ),
        out_specs=(P("stream", "tp"), P("stream", "tp", None, None)),
        check_vma=False,
    )
```
